32 devices in a mesh: wide: 8 (over z, x), narrow: 4 (over y, core).
Axes of the slice: x: 2, y: 2, z: 4, core: 2. Of those that a mesh axis runs over, the one named last changes fastest.
Arguments:
- features: bfloat16 [18816, 2048], P('wide', 'narrow')
- image_side: int32 [384], P('wide'), may hold values from 5 to 7, as said below
- bank_slot: int32 [384], P('wide'), may hold values from 0 to 32767, as said below
- memory_bank: float32 [32768, 128], P('wide'), may hold values from -0.6 to 0.6
- weight_one: bfloat16 [2048, 512], P(None, 'narrow'), may hold values from -0.125 to 0.125
- gain_one: bfloat16 [512], P('narrow'), may hold values from 0.5 to 1.5
- shift_one: bfloat16 [512], P('narrow'), may hold values from -2 to 2
- weight_two: bfloat16 [3, 3, 512, 512], P(None, None, None, 'narrow'), may hold values from -0.09375 to 0.09375
- gain_two: bfloat16 [512], P('narrow'), may hold values from 0.5 to 1.5
- shift_two: bfloat16 [512], P('narrow'), may hold values from -2 to 2
- weight_three: bfloat16 [512, 2048], P(None, 'narrow'), may hold values from -0.25 to 0.25
- gain_three: bfloat16 [2048], P('narrow'), may hold values from 0.5 to 1.5
- shift_three: bfloat16 [2048], P('narrow'), may hold values from -2 to 2
- weight_head: bfloat16 [2048, 128], P('narrow'), may hold values from -0.125 to 0.125
- out_grad: bfloat16 [18816, 2048], P('wide', 'narrow'), may hold values from -6 to 6
- embed_grad: float32 [384, 128], P('wide'), may hold values from -6 to 6
Outputs:
- out: bfloat16 [18816, 2048], P('wide', 'narrow')
- embedding: float32 [384, 128], P('wide')
- grad_features: bfloat16 [18816, 2048], P('wide', 'narrow')
- grad_weight_one: float32 [2048, 512], P(None, 'narrow')
- grad_gain_one: float32 [512], P('narrow')
- grad_shift_one: float32 [512], P('narrow')
- grad_weight_two: float32 [3, 3, 512, 512], P(None, None, None, 'narrow')
- grad_gain_two: float32 [512], P('narrow')
- grad_shift_two: float32 [512], P('narrow')
- grad_weight_three: float32 [512, 2048], P(None, 'narrow')
- grad_gain_three: float32 [2048], P('narrow')
- grad_shift_three: float32 [2048], P('narrow')
- grad_weight_head: float32 [2048, 128], P('narrow')
- new_bank: float32 [32768, 128], P('wide')
The draws below stay inside these ranges and needn't reach their ends.
Inputs may be any that keep to these rules, and one draw needn't show every extreme that they name: `image_side`: all images of one index of wide have the same side. `bank_slot`: the 384 rows are all different.
All inputs are finite; a program needn't handle non-finite values.
Results may differ from the reference program's by a relative error of at most 0.009.
Values may be sent and summed in bfloat16 or wider, within the bound.
No kernel may reach another device: no remote copies, remote signals or barrier semaphores. Data moves between devices by JAX's collectives and lax.ppermute only.
A program may use at most 192 MiB of HBM per device.

```python
import jax
import jax.numpy as jnp
from jax import lax

C_IN = 2048
C_MID = 512
EMB = 128
SIDE = 7
IMG_DEV = 48
IMAGES = 384
PIXELS = 18816
BANK = 32768


def draw_features(key, part):
    image_of_row = (jnp.arange(PIXELS, dtype=jnp.int32) // (SIDE * SIDE)).astype(jnp.float32)
    level = jnp.exp(jnp.log(3.0) * image_of_row / IMAGES)[:, None]
    base = jax.random.normal(key, (PIXELS, C_IN), jnp.float32) * level
    return base.astype(jnp.bfloat16)


def draw_image_side(key, part):
    groups = IMAGES // IMG_DEV
    chosen = jax.random.randint(key, (groups,), 5, 8)
    chosen = chosen.at[0].set(7).at[groups - 1].set(5)
    return jnp.repeat(chosen, IMG_DEV, total_repeat_length=IMAGES).astype(jnp.int32)


def draw_bank_slot(key, part):
    order = jax.random.permutation(jax.random.fold_in(key, 11), BANK)
    lowest_at = jnp.argmin(order)
    order = order.at[lowest_at].set(order[0]).at[0].set(0)
    highest_at = jnp.argmax(order)
    order = order.at[highest_at].set(order[1]).at[1].set(BANK - 1)
    chosen = order[:IMAGES]
    return jax.random.permutation(jax.random.fold_in(key, 12), chosen).astype(jnp.int32)


def block_scale(rng, dims, shards, smallest, high):
    loudness, own = 1.0, jax.random.fold_in(rng, 6)
    for axis_at, shards_of in shards:
        draws = jnp.exp(jax.random.uniform(jax.random.fold_in(own, axis_at), (shards_of,), jnp.float32, smallest / len(shards), high / len(shards)))
        loudness = loudness * jnp.repeat(draws, dims[axis_at] // shards_of).reshape([-1 if axis == axis_at else 1 for axis in range(len(dims))])
    return loudness


def normal_values(stream_key, extent, spread, most, cuts=(), held_as=jnp.bfloat16):
    factor_of = block_scale(stream_key, extent, cuts, -0.22, 0.18) if cuts else 1.0
    values = jax.random.normal(stream_key, extent, jnp.float32) * spread * factor_of
    return jnp.minimum(jnp.maximum(values, -most), most).astype(held_as)


def setup_inputs(seed: int = 0) -> dict:
    seeds = jax.random.split(jax.random.key(seed), 17)
    features = draw_features(jax.random.fold_in(seeds[16], 71), 0)
    image_side = draw_image_side(jax.random.fold_in(seeds[16], 71), 0)
    bank_slot = draw_bank_slot(jax.random.fold_in(seeds[16], 71), 0)
    memory_bank = normal_values(seeds[3], (BANK, EMB), 0.088, 0.6, ((0, 8),), jnp.float32)
    weight_one = normal_values(seeds[4], (C_IN, C_MID), C_IN ** -0.5, 0.125, ((1, 4),))
    gain_one = jnp.clip(0.5 + 1.0 * jax.random.uniform(seeds[5], (C_MID,), jnp.float32) ** block_scale(seeds[5], (C_MID,), ((0, 4),), -0.2, 0.2), 0.5, 1.5).astype(jnp.bfloat16)
    shift_one = normal_values(seeds[6], (C_MID,), 0.5, 2.0, ((0, 4),))
    weight_two = normal_values(seeds[7], (3, 3, C_MID, C_MID), (9 * C_MID) ** -0.5, 0.09375, ((3, 4),))
    gain_two = jnp.clip(0.5 + 1.0 * jax.random.uniform(seeds[8], (C_MID,), jnp.float32) ** block_scale(seeds[8], (C_MID,), ((0, 4),), -0.2, 0.2), 0.5, 1.5).astype(jnp.bfloat16)
    shift_two = normal_values(seeds[9], (C_MID,), 0.5, 2.0, ((0, 4),))
    weight_three = normal_values(seeds[10], (C_MID, C_IN), C_MID ** -0.5, 0.25, ((1, 4),))
    gain_three = jnp.clip(0.5 + 1.0 * jax.random.uniform(seeds[11], (C_IN,), jnp.float32) ** block_scale(seeds[11], (C_IN,), ((0, 4),), -0.2, 0.2), 0.5, 1.5).astype(jnp.bfloat16)
    shift_three = normal_values(seeds[12], (C_IN,), 0.5, 2.0, ((0, 4),))
    weight_head = normal_values(seeds[13], (C_IN, EMB), C_IN ** -0.5, 0.125, ((0, 4),))
    out_grad = normal_values(seeds[14], (PIXELS, C_IN), 1.0, 6.0, ((0, 8), (1, 4)))
    embed_grad = normal_values(seeds[15], (IMAGES, EMB), 1.0, 6.0, ((0, 8),), jnp.float32)
    return {"features": features, "image_side": image_side, "bank_slot": bank_slot, "memory_bank": memory_bank, "weight_one": weight_one, "gain_one": gain_one, "shift_one": shift_one, "weight_two": weight_two, "gain_two": gain_two, "shift_two": shift_two, "weight_three": weight_three, "gain_three": gain_three, "shift_three": shift_three, "weight_head": weight_head, "out_grad": out_grad, "embed_grad": embed_grad}


@jax.custom_vjp
def low(v):
    return lax.optimization_barrier(v.astype(jnp.bfloat16)).astype(jnp.float32)

@jax.custom_vjp
def low_back(v):
    return v

def low_keep(v):
    return (low(v), None)

def low_pass(kept, grad):
    return (grad,)

def back_keep(v):
    return (v, None)

def back_low(kept, grad):
    return (low(grad),)
low.defvjp(low_keep, low_pass)
low_back.defvjp(back_keep, back_low)
EPS_NORM = 1e-05
EPS_EMBED = 1e-06
highest = lax.Precision.HIGHEST

def pixel_mask(image_side):
    position = jnp.arange(SIDE * SIDE, dtype=jnp.int32)
    row_index = position // SIDE
    column_index = position % SIDE
    inside = (row_index[None, :] < image_side[:, None]) & (column_index[None, :] < image_side[:, None])
    return inside.astype(jnp.float32).reshape(-1, 1)

def matmul(left, right):
    return jnp.dot(left, right, precision=highest)

def batch_norm(value, gain, shift, mask, count):
    mean = lax.optimization_barrier(jnp.sum(value * mask, axis=0)) / count
    variance = lax.optimization_barrier(jnp.sum(value * value * mask, axis=0)) / count - mean * mean
    return gain * (value - mean) * lax.rsqrt(variance + EPS_NORM) + shift

def conv_three(value, weight, images):
    channels = value.shape[1]
    padded = jnp.pad(value.reshape(images, SIDE, SIDE, channels), ((0, 0), (1, 1), (1, 1), (0, 0)))
    total = jnp.zeros((value.shape[0], weight.shape[3]), jnp.float32)
    for row_shift in range(3):
        for column_shift in range(3):
            window = padded[:, row_shift:row_shift + SIDE, column_shift:column_shift + SIDE].reshape(-1, channels)
            total = total + matmul(window, weight[row_shift, column_shift])
    return total

def forward(features, weight_one, gain_one, shift_one, weight_two, gain_two, shift_two, weight_three, gain_three, shift_three, weight_head, mask, counts_img, count):
    images = counts_img.shape[0]
    masked = features * mask
    y_one = low_back(matmul(masked, weight_one))
    a_one = low(jax.nn.silu(batch_norm(y_one, gain_one, shift_one, mask, count)) * mask)
    y_two = low_back(conv_three(a_one, weight_two, images))
    a_two = low(jax.nn.silu(batch_norm(y_two, gain_two, shift_two, mask, count)) * mask)
    y_three = low_back(matmul(a_two, weight_three))
    out_full = jax.nn.silu(batch_norm(y_three, gain_three, shift_three, mask, count) + masked) * mask
    channels = out_full.shape[1]
    pooled = low(lax.optimization_barrier(jnp.sum(out_full.reshape(images, SIDE * SIDE, channels), axis=1)) / counts_img[:, None])
    raw = low_back(matmul(pooled, weight_head))
    embedding = raw * lax.rsqrt(lax.optimization_barrier(jnp.sum(raw * raw, axis=1, keepdims=True)) + EPS_EMBED)
    return (out_full, embedding)

def reference(features, image_side, bank_slot, memory_bank, weight_one, gain_one, shift_one, weight_two, gain_two, shift_two, weight_three, gain_three, shift_three, weight_head, out_grad, embed_grad):
    mask = pixel_mask(image_side)
    counts_img = (image_side * image_side).astype(jnp.float32)
    count = jnp.sum(counts_img)
    params = tuple((value.astype(jnp.float32) for value in (features, weight_one, gain_one, shift_one, weight_two, gain_two, shift_two, weight_three, gain_three, shift_three, weight_head)))

    def run(*values):
        return forward(*values, mask, counts_img, count)
    (out_full, embedding), pullback = jax.vjp(run, *params)
    grads = pullback((out_grad.astype(jnp.float32), embed_grad))
    previous = memory_bank[bank_slot]
    mixed = 0.5 * previous + 0.5 * embedding
    mixed = mixed * lax.rsqrt(lax.optimization_barrier(jnp.sum(mixed * mixed, axis=1, keepdims=True)) + EPS_EMBED)
    new_bank = memory_bank.at[bank_slot].set(mixed)
    return (out_full.astype(jnp.bfloat16), embedding, grads[0].astype(jnp.bfloat16), grads[1], grads[2], grads[3], grads[4], grads[5], grads[6], grads[7], grads[8], grads[9], grads[10], new_bank)
```

```python
import functools

import jax
import jax.numpy as jnp
import numpy as np
from jax import lax
from jax.experimental import pallas as pl
from jax.experimental.pallas import tpu as pltpu
from jax.sharding import Mesh
from jax.sharding import PartitionSpec as P

SIDE = 7
SLOTS = SIDE * SIDE
GROUP = 8
ROWS = GROUP * SLOTS
EPS_NORM = 1e-05
EPS_EMBED = 1e-06
F32 = jnp.float32
BF16 = jnp.bfloat16
LANES = 128
OFFSETS = [(i - 1) * SIDE + (j - 1) for i in range(3) for j in range(3)]
ALL = ("wide", "hi", "lo")
VMEM_BYTES = 56 * 1024 * 1024


def tap_masks():
    row = (np.arange(ROWS) % SLOTS) // SIDE
    column = np.arange(ROWS) % SIDE
    kept = np.zeros((ROWS, 9), np.float32)
    for i in range(3):
        for j in range(3):
            r, c = row + i - 1, column + j - 1
            kept[:, 3 * i + j] = (r >= 0) & (r < SIDE) & (c >= 0) & (c < SIDE)
    return kept


def image_rows():
    image = np.arange(ROWS) // SLOTS
    return (image[None, :] == np.arange(GROUP)[:, None]).astype(np.float32)


def swap_lo(value):
    return lax.ppermute(value, "lo", [(0, 1), (1, 0)])


def swap_hi(value):
    return lax.ppermute(value, "hi", [(0, 1), (1, 0)])


def swap_both(value):
    return lax.ppermute(value, ("hi", "lo"), [(i, i ^ 3) for i in range(4)])


def spread(value, axes, copies):
    return lax.all_to_all(
        jnp.broadcast_to(value[None], (copies,) + value.shape), axes, 0, 0, tiled=True
    )


def sigmoid(value):
    return 1.0 / (1.0 + jnp.exp(-value))


def slope_of(value, sigma):
    return sigma * (1.0 + value * (1.0 - sigma))


def dot(left, right):
    return jnp.dot(left, right, preferred_element_type=F32)


def dot_nt(left, right):
    return lax.dot_general(left, right, (((1,), (1,)), ((), ())), preferred_element_type=F32)


def dot_tn(left, right):
    return lax.dot_general(left, right, (((0,), (0,)), ((), ())), preferred_element_type=F32)


def total_count(e_ref):
    e = e_ref[...]
    return jnp.sum(e.reshape(-1, 4, 8, LANES)[:, 0, 4:5, :], axis=0)


def set_sums(r_ref):
    r = r_ref[...]
    by_narrow = jnp.sum(r.reshape(-1, 4, 4, LANES), axis=0)
    sets = [by_narrow[k] + by_narrow[2 + k] for k in range(2)]
    return [(s[0:2], s[2:4]) for s in sets]


def flat(rows):
    return jnp.concatenate([rows[k : k + 1] for k in range(rows.shape[0])], axis=1)


def unflat(vector):
    return jnp.concatenate(
        [vector[:, k * LANES : (k + 1) * LANES] for k in range(vector.shape[1] // LANES)], axis=0
    )


class Norm:
    def __init__(self, sums, squares, count, gain, shift):
        self.mean = sums / count
        variance = squares / count - self.mean * self.mean
        self.scale = lax.rsqrt(variance + EPS_NORM)
        self.gain = gain
        self.shift = shift

    def normal(self, value):
        return (value - self.mean) * self.scale

    def apply(self, value):
        return self.gain * self.normal(value) + self.shift


def gains_of(e_ref, core, at):
    return jnp.concatenate([e_ref[core, at : at + 1], e_ref[2 + core, at : at + 1]], axis=1)


def mid_norms(e_ref, r_ref, at):
    count = total_count(e_ref)[:, :1]
    sums = set_sums(r_ref)
    return [
        Norm(
            flat(sums[core][0]),
            flat(sums[core][1]),
            count,
            gains_of(e_ref, core, at),
            gains_of(e_ref, core, at + 1),
        )
        for core in range(2)
    ], count


def choose(flag, first, second):
    return jnp.where(flag, first, second)


def choose_norm(flag, first, second):
    out = Norm.__new__(Norm)
    for name in ("mean", "scale", "gain", "shift"):
        setattr(out, name, jnp.where(flag, getattr(first, name), getattr(second, name)))
    return out


def half_norm(norm, second):
    out = Norm.__new__(Norm)
    for name in ("mean", "scale", "gain", "shift"):
        v = getattr(norm, name)
        setattr(out, name, jnp.where(second, v[:, LANES:], v[:, :LANES]))
    return out


def natural(set0, set1):
    return jnp.concatenate(
        [set0[:, :LANES], set1[:, :LANES], set0[:, LANES:], set1[:, LANES:]], axis=1
    )


def sets_of(value):
    return (
        jnp.concatenate([value[:, :LANES], value[:, 2 * LANES : 3 * LANES]], axis=1),
        jnp.concatenate([value[:, LANES : 2 * LANES], value[:, 3 * LANES :]], axis=1),
    )


def add_sums(st_ref, first, second, step):
    rows = jnp.concatenate([unflat(first), unflat(second)], axis=0)

    @pl.when(step == 0)
    def _():
        st_ref[...] = rows

    @pl.when(step > 0)
    def _():
        st_ref[...] += rows


def whole(shape):
    zero = (0,) * len(shape)
    return pl.BlockSpec(shape, lambda i, *_: zero)


def rows_spec(width, pick=None):
    if pick is None:
        return pl.BlockSpec((ROWS, width), lambda i, *_: (i, 0))
    return pl.BlockSpec((ROWS, width), pick)


def call(kernel, steps, in_specs, out_specs, out_shape, scratch=(), flops=0, bytes_moved=0, name=None):
    return pl.pallas_call(
        kernel,
        grid_spec=pltpu.PrefetchScalarGridSpec(
            num_scalar_prefetch=1,
            grid=(steps,),
            in_specs=in_specs,
            out_specs=out_specs,
            scratch_shapes=scratch,
        ),
        out_shape=out_shape,
        compiler_params=pltpu.CompilerParams(
            dimension_semantics=("arbitrary",), vmem_limit_bytes=VMEM_BYTES
        ),
        cost_estimate=pl.CostEstimate(flops=flops, bytes_accessed=bytes_moved, transcendentals=0),
        name=name,
    )


def one_kernel(at_ref, keep_ref, near_ref, far_ref, y_ref, st_ref):
    value = keep_ref[...] + near_ref[...].astype(F32) + far_ref[...].astype(F32)
    y_ref[...] = value.astype(BF16)
    add_sums(
        st_ref,
        jnp.sum(value, axis=0, keepdims=True),
        jnp.sum(value * value, axis=0, keepdims=True),
        pl.program_id(0),
    )


def conv_forward_kernel(at_ref, e_ref, r_ref, own_ref, near_ref, w_ref, mk_ref, y_ref, st_ref):
    norms, _ = mid_norms(e_ref, r_ref, 0)
    lo0 = at_ref[1] == 0
    inside = mk_ref[:, 9:10]
    own, near = own_ref[...].astype(F32), near_ref[...].astype(F32)
    halves = []
    for core in range(2):
        z = norms[core].apply(choose(lo0 if core == 0 else jnp.logical_not(lo0), own, near))
        halves.append(jnp.where(inside > 0, z * sigmoid(z), 0.0).astype(BF16))
    a = natural(halves[0], halves[1])
    total = jnp.zeros((ROWS, 2 * LANES), F32)
    for tap, offset in enumerate(OFFSETS):
        part = dot(a, w_ref[tap])
        if offset:
            part = pltpu.roll(part, (-offset) % ROWS, 0)
        total = total + part * mk_ref[:, tap : tap + 1]
    y_ref[...] = total.astype(BF16)
    kept = total * inside
    add_sums(
        st_ref,
        jnp.sum(kept, axis=0, keepdims=True),
        jnp.sum(kept * total, axis=0, keepdims=True),
        pl.program_id(0),
    )


def select_blocks(at_ref, refs, step, per_half):
    own, near, far, across = [ref[...].astype(F32) for ref in refs]
    mine = (step // per_half) == at_ref[0]
    a, b = choose(mine, own, far), choose(mine, near, across)
    lo0 = at_ref[1] == 0
    return choose(lo0, a, b), choose(lo0, b, a)


def third_kernel(per_half, at_ref, e_ref, r_ref, b0, b1, b2, b3, w_ref, mk_ref, a_ref, y_ref, st_ref):
    step = pl.program_id(0)
    norms, _ = mid_norms(e_ref, r_ref, 2)
    inside = mk_ref[:, 9:10]
    halves = []
    for norm, value in zip(norms, select_blocks(at_ref, (b0, b1, b2, b3), step, per_half)):
        z = norm.apply(value)
        halves.append(jnp.where(inside > 0, z * sigmoid(z), 0.0).astype(BF16))
    a = natural(halves[0], halves[1])
    a_ref[...] = a
    y = dot(a, w_ref[...])
    y_ref[...] = y
    add_sums(
        st_ref, jnp.sum(y, axis=0, keepdims=True), jnp.sum(y * y, axis=0, keepdims=True), step
    )


def third_norm(e_ref, r_ref, gb_ref):
    count = total_count(e_ref)[:, :1]
    sums = jnp.sum(r_ref[...], axis=0)
    return Norm(flat(sums[0:4]), flat(sums[4:8]), count, flat(gb_ref[0:4]), flat(gb_ref[4:8])), count


def split_low(value):
    high = value.astype(BF16)
    return high, (value - high.astype(F32)).astype(BF16)


def out_kernel(
    at_ref, e_ref, r_ref, gb_ref, y_ref, x_ref, og_ref, mk_ref, ind_ref, wh_ref,
    out_ref, pool_ref, s0_ref, s1_ref, raw_ref, st_ref,
):
    norm, _ = third_norm(e_ref, r_ref, gb_ref)
    inside = mk_ref[:, 9:10] > 0
    normal = norm.normal(y_ref[...])
    summed = jnp.where(
        inside, norm.gain * normal + norm.shift + x_ref[...].astype(F32), 0.0
    )
    sigma = sigmoid(summed)
    out = summed * sigma
    slope = jnp.where(inside, slope_of(summed, sigma), 0.0)
    out_ref[...] = out.astype(BF16)
    ind = ind_ref[...]
    high, low = split_low(out)
    pooled = ((dot(ind, high) + dot(ind, low)) / mk_ref[0:GROUP, 10:11]).astype(BF16)
    pool_ref[...] = pooled.astype(F32)
    sloped = slope * normal
    s0_ref[...] = dot(ind, slope.astype(BF16))
    s1_ref[...] = dot(ind, sloped.astype(BF16))
    raw_ref[...] = dot(pooled, wh_ref[...])
    og = og_ref[...].astype(F32)
    add_sums(
        st_ref,
        jnp.sum(og * slope, axis=0, keepdims=True),
        jnp.sum(og * sloped, axis=0, keepdims=True),
        pl.program_id(0),
    )


def head_kernel(
    at_ref, raw_ref, eg_ref, wh_ref, s0_ref, s1_ref, stl_ref, mk_ref,
    emb_ref, graw_ref, gp_ref, st_ref,
):
    raw, eg = raw_ref[...], eg_ref[...]
    inverse = lax.rsqrt(jnp.sum(raw * raw, axis=1, keepdims=True) + EPS_EMBED)
    emb = raw * inverse
    graw = (inverse * (eg - emb * jnp.sum(emb * eg, axis=1, keepdims=True))).astype(BF16)
    emb_ref[...] = emb
    graw_ref[...] = graw.astype(F32)
    gp = dot_nt(graw, wh_ref[...]) / mk_ref[0:1, 10:11]
    gp_ref[...] = gp
    add = jnp.concatenate(
        [
            unflat(jnp.sum(gp * s0_ref[...], axis=0, keepdims=True)),
            unflat(jnp.sum(gp * s1_ref[...], axis=0, keepdims=True)),
        ],
        axis=0,
    )
    st_ref[...] = stl_ref[...] + add


def back_three_kernel(
    at_ref, e_ref, r_ref, rb_ref, gb_ref, y_ref, x_ref, og_ref, gp_ref, mk_ref, ind_ref, w_ref,
    keep_ref, send_ref, gy_ref, dz_ref,
):
    norm, count = third_norm(e_ref, r_ref, gb_ref)
    back = jnp.sum(rb_ref[...], axis=0)
    d_shift, d_gain = flat(back[0:4]) / count, flat(back[4:8]) / count
    inside = mk_ref[:, 9:10] > 0
    normal = norm.normal(y_ref[...])
    summed = norm.gain * normal + norm.shift + x_ref[...].astype(F32)
    slope = jnp.where(inside, slope_of(summed, sigmoid(summed)), 0.0)
    high, low = split_low(gp_ref[...])
    ind = ind_ref[...]
    given = og_ref[...].astype(F32) + dot_tn(ind, high) + dot_tn(ind, low)
    dz = given * slope
    dz_ref[...] = dz.astype(BF16)
    gy = norm.gain * norm.scale * (dz - d_shift - normal * d_gain)
    gy = jnp.where(inside, gy, 0.0).astype(BF16)
    gy_ref[...] = gy
    set0, set1 = sets_of(dot_nt(gy, w_ref[...]))
    lo0 = at_ref[1] == 0
    keep_ref[...] = choose(lo0, set0, set1)
    send_ref[...] = choose(lo0, set1, set0).astype(BF16)


def slope_kernel(at, parts, at_ref, e_ref, r_ref, *refs):
    given, (y_ref, mk_ref, dz_ref, st_ref) = refs[:parts], refs[parts:]
    norms, _ = mid_norms(e_ref, r_ref, at)
    norm = choose_norm(at_ref[1] == 0, norms[0], norms[1])
    value = given[0][...].astype(F32)
    for ref in given[1:]:
        value = value + ref[...].astype(F32)
    normal = norm.normal(y_ref[...].astype(F32))
    z = norm.gain * normal + norm.shift
    dz = jnp.where(mk_ref[:, 9:10] > 0, value * slope_of(z, sigmoid(z)), 0.0)
    dz_ref[...] = dz.astype(BF16)
    add_sums(
        st_ref,
        jnp.sum(dz, axis=0, keepdims=True),
        jnp.sum(dz * normal, axis=0, keepdims=True),
        pl.program_id(0),
    )


def set_back(rb_ref, count):
    sums = set_sums(rb_ref)
    return [(flat(s[0]) / count, flat(s[1]) / count) for s in sums]


def grad_y(norm, dz, value, back, inside):
    gy = norm.gain * norm.scale * (dz - back[0] - norm.normal(value) * back[1])
    return jnp.where(inside, gy, 0.0)


def conv_input_kernel(
    at_ref, e_ref, r_ref, rb_ref, dz_ref, y_ref, w_ref, mk_ref, keep_ref, send_ref
):
    norms, count = mid_norms(e_ref, r_ref, 2)
    lo0 = at_ref[1] == 0
    norm = choose_norm(lo0, norms[0], norms[1])
    backs = set_back(rb_ref, count)
    back = [choose(lo0, backs[0][k], backs[1][k]) for k in range(2)]
    gy = grad_y(
        norm, dz_ref[...].astype(F32), y_ref[...].astype(F32), back, mk_ref[:, 9:10] > 0
    ).astype(BF16).astype(F32)
    total = jnp.zeros((ROWS, 4 * LANES), F32)
    for tap, offset in enumerate(OFFSETS):
        moved = pltpu.roll(gy, offset % ROWS, 0) if offset else gy
        moved = (moved * mk_ref[:, 8 - tap : 9 - tap]).astype(BF16)
        total = total + dot_nt(moved, w_ref[tap])
    set0, set1 = sets_of(total)
    keep_ref[...] = choose(lo0, set0, set1)
    send_ref[...] = choose(lo0, set1, set0).astype(BF16)


def conv_weight_kernel(
    per_half, at_ref, e_ref, r1_ref, r2_ref, rb_ref, b0, b1, b2, b3, dzo_ref, dzf_ref,
    yo_ref, yf_ref, mk_ref, gw_ref, acc_ref,
):
    step = pl.program_id(0)
    inside = mk_ref[:, 9:10]
    ones, count = mid_norms(e_ref, r1_ref, 0)
    halves = []
    for norm, value in zip(ones, select_blocks(at_ref, (b0, b1, b2, b3), step, per_half)):
        z = norm.apply(value)
        halves.append(jnp.where(inside > 0, z * sigmoid(z), 0.0).astype(BF16))
    a = natural(halves[0], halves[1])
    norms, _ = mid_norms(e_ref, r2_ref, 2)
    lo0, second = at_ref[1] == 0, at_ref[0] == 1
    norm = half_norm(choose_norm(lo0, norms[0], norms[1]), second)
    backs = set_back(rb_ref, count)
    back = [choose(lo0, backs[0][k], backs[1][k]) for k in range(2)]
    back = [choose(second, v[:, LANES:], v[:, :LANES]) for v in back]
    mine = (step // per_half) == at_ref[0]
    dz = choose(mine, dzo_ref[...].astype(F32), dzf_ref[...].astype(F32))
    y = choose(mine, yo_ref[...].astype(F32), yf_ref[...].astype(F32))
    gy = grad_y(norm, dz, y, back, inside > 0).astype(BF16).astype(F32)
    moved = []
    for tap, offset in enumerate(OFFSETS):
        part = pltpu.roll(gy, offset % ROWS, 0) if offset else gy
        moved.append((part * mk_ref[:, 8 - tap : 9 - tap]).astype(BF16))
    part = dot_tn(a, jnp.concatenate(moved, axis=1))

    @pl.when(step == 0)
    def _():
        acc_ref[...] = part

    @pl.when(step > 0)
    def _():
        acc_ref[...] += part

    @pl.when(step == pl.num_programs(0) - 1)
    def _():
        for tap in range(9):
            gw_ref[tap] = acc_ref[:, tap * LANES : (tap + 1) * LANES].astype(BF16)


def first_weight_kernel(
    per_half, at_ref, e_ref, r_ref, rb_ref, d0, d1, d2, d3, b0, b1, b2, b3, x_ref, mk_ref,
    gy_ref, gw_ref, acc_ref,
):
    step = pl.program_id(0)
    norms, count = mid_norms(e_ref, r_ref, 0)
    backs = set_back(rb_ref, count)
    inside = mk_ref[:, 9:10] > 0
    dzs = select_blocks(at_ref, (d0, d1, d2, d3), step, per_half)
    ys = select_blocks(at_ref, (b0, b1, b2, b3), step, per_half)
    halves = [
        grad_y(norms[k], dzs[k], ys[k], backs[k], inside).astype(BF16) for k in range(2)
    ]
    gy = natural(halves[0], halves[1])
    gy_ref[...] = gy
    part = dot_tn(x_ref[...], gy)

    @pl.when(step == 0)
    def _():
        acc_ref[...] = part

    @pl.when(step > 0)
    def _():
        acc_ref[...] += part

    @pl.when(step == pl.num_programs(0) - 1)
    def _():
        for block in range(4):
            gw_ref[block] = acc_ref[:, block * LANES : (block + 1) * LANES].astype(BF16)


def shards(
    n_wide,
    features,
    image_side,
    bank_slot,
    memory_bank,
    weight_one,
    gain_one,
    shift_one,
    weight_two,
    gain_two,
    shift_two,
    weight_three,
    gain_three,
    shift_three,
    weight_head,
    out_grad,
    embed_grad,
):
    hi, lo = lax.axis_index("hi"), lax.axis_index("lo")
    at = jnp.stack([hi, lo]).astype(jnp.int32)
    pixels, width = features.shape
    images = image_side.shape[0]
    half = pixels // 2
    per_half = half // ROWS
    steps = 2 * per_half
    n_all = 4 * n_wide
    hi0, lo0 = hi == 0, lo == 0
    side = image_side[0]

    position = jnp.arange(ROWS, dtype=jnp.int32)
    inside = (((position % SLOTS) // SIDE) < side) & ((position % SIDE) < side)
    count_img = (side * side).astype(F32)
    mk = jnp.concatenate(
        [
            jnp.asarray(tap_masks()),
            inside.astype(F32)[:, None],
            jnp.full((ROWS, 6), count_img, F32),
        ],
        axis=1,
    )
    ind = jnp.asarray(image_rows(), BF16)
    mk_spec, ind_spec = whole((ROWS, 16)), whole((GROUP, ROWS))
    e_spec, r_spec = whole((n_all, 8, LANES)), whole((n_all, 4, LANES))
    r3_spec, st_spec = whole((n_wide, 8, LANES)), whole((4, LANES))
    st_shape = jax.ShapeDtypeStruct((4, LANES), F32)

    rows_of = lambda h, l: lax.dynamic_slice_in_dim(weight_one, (2 * h + l) * width, width, 0)
    w_self = rows_of(hi, lo)
    w_near = swap_lo(rows_of(hi, 1 - lo))
    w_far = swap_hi(rows_of(1 - hi, lo))
    w_across = swap_both(rows_of(1 - hi, 1 - lo))

    small = jnp.concatenate(
        [
            gain_one.astype(F32)[None],
            shift_one.astype(F32)[None],
            gain_two.astype(F32)[None],
            shift_two.astype(F32)[None],
            jnp.full((1, LANES), count_img * images, F32),
            jnp.pad(bank_slot.astype(F32), (0, LANES - images))[None],
            jnp.zeros((2, LANES), F32),
        ],
        axis=0,
    )
    every = spread(small, ALL, n_all)
    gb3 = jnp.concatenate(
        [gain_three.astype(F32).reshape(4, LANES), shift_three.astype(F32).reshape(4, LANES)], 0
    )

    w_own = jnp.concatenate([jnp.where(hi0, w_self, w_far), jnp.where(hi0, w_far, w_self)], 1)
    w_oth = jnp.concatenate([jnp.where(hi0, w_near, w_across), jnp.where(hi0, w_across, w_near)], 1)
    w_set0, w_set1 = jnp.where(lo0, w_own, w_oth), jnp.where(lo0, w_oth, w_own)
    w_first = natural(w_set0, w_set1)
    w2_far = swap_hi(weight_two)
    w2 = jnp.concatenate(
        [jnp.where(hi0, weight_two, w2_far), jnp.where(hi0, w2_far, weight_two)], axis=3
    ).reshape(9, weight_two.shape[2], 2 * LANES)

    pixel_inside = jnp.tile(inside, steps)[:, None]
    masked = jnp.where(pixel_inside, features, jnp.zeros_like(features))
    near = swap_lo(dot(masked, w_oth).astype(BF16))
    keep = dot(masked, w_own)
    other_rows = (1 - hi) * half
    pick = lambda v: lax.dynamic_slice_in_dim(v, other_rows, half, 0)
    far = swap_hi((pick(keep) + pick(near).astype(F32)).astype(BF16))
    own_spec = rows_spec(2 * LANES, lambda i, at: (at[0] * per_half + i, 0))
    row_spec = rows_spec(2 * LANES)
    y_shape = jax.ShapeDtypeStruct((half, 2 * LANES), BF16)
    y1, st1 = call(
        one_kernel, per_half, [own_spec, own_spec, row_spec], [row_spec, st_spec],
        [y_shape, st_shape], bytes_moved=4 << 20, name="one",
    )(at, keep, near, far)
    y1_near = swap_lo(y1)
    r1 = spread(st1, ALL, n_all)

    w2_spec = whole(w2.shape)
    y2, st2 = call(
        conv_forward_kernel, per_half,
        [e_spec, r_spec, row_spec, row_spec, w2_spec, mk_spec], [row_spec, st_spec],
        [y_shape, st_shape], flops=18 * half * 512 * 256, bytes_moved=6 << 20, name="conv_forward",
    )(at, every, r1, y1, y1_near, w2, mk)
    y2_near = swap_lo(y2)
    y2_far = swap_hi(y2)
    r2 = spread(st2, ALL, n_all)
    y2_across = swap_lo(y2_far)

    y1_far = swap_hi(y1)
    y1_across = swap_lo(y1_far)

    part_spec = rows_spec(2 * LANES, lambda i, at: (i % per_half, 0))
    parts = [part_spec] * 4
    wide_spec = rows_spec(width)
    a2, y3, st3 = call(
        functools.partial(third_kernel, per_half), steps,
        [e_spec, r_spec] + parts + [whole(weight_three.shape), mk_spec],
        [wide_spec, wide_spec, whole((8, LANES))],
        [
            jax.ShapeDtypeStruct((pixels, 4 * LANES), BF16),
            jax.ShapeDtypeStruct((pixels, width), F32),
            jax.ShapeDtypeStruct((8, LANES), F32),
        ],
        flops=2 * pixels * 512 * width, bytes_moved=10 << 20, name="third",
    )(at, every, r2, y2, y2_near, y2_far, y2_across, weight_three, mk)
    r3 = spread(st3, "wide", n_wide)

    img_spec = pl.BlockSpec((GROUP, width), lambda i, *_: (i, 0))
    img_shape = jax.ShapeDtypeStruct((images, width), F32)
    gb_spec = whole((8, LANES))
    head_spec = whole(weight_head.shape)
    out, pooled, s0, s1, raw, st_local = call(
        out_kernel, steps,
        [e_spec, r3_spec, gb_spec, wide_spec, wide_spec, wide_spec, mk_spec, ind_spec, head_spec],
        [wide_spec, img_spec, img_spec, img_spec, pl.BlockSpec((GROUP, LANES), lambda i, *_: (i, 0)), whole((8, LANES))],
        [
            jax.ShapeDtypeStruct((pixels, width), BF16), img_shape, img_shape, img_shape,
            jax.ShapeDtypeStruct((images, LANES), F32), jax.ShapeDtypeStruct((8, LANES), F32),
        ],
        flops=8 * pixels * width, bytes_moved=12 << 20, name="out",
    )(at, every, r3, gb3, y3, features, out_grad, mk, ind, weight_head)
    raw = raw + swap_lo(raw)
    raw = raw + swap_hi(raw)
    small_spec = whole((images, LANES))
    all_img = whole((images, width))
    embedding, grad_raw, grad_pooled, st3b = call(
        head_kernel, 1,
        [small_spec, small_spec, head_spec, all_img, all_img, whole((8, LANES)), mk_spec],
        [small_spec, small_spec, all_img, whole((8, LANES))],
        [
            jax.ShapeDtypeStruct((images, LANES), F32), jax.ShapeDtypeStruct((images, LANES), F32),
            img_shape, jax.ShapeDtypeStruct((8, LANES), F32),
        ],
        bytes_moved=1 << 19, name="head",
    )(at, raw, embed_grad, weight_head, s0, s1, st_local, mk)
    r3b = spread(st3b, "wide", n_wide)

    set_spec = rows_spec(2 * LANES)
    ga_keep, ga_send, gy3, dz3 = call(
        back_three_kernel, steps,
        [e_spec, r3_spec, r3_spec, gb_spec, wide_spec, wide_spec, wide_spec, img_spec, mk_spec, ind_spec, whole(weight_three.shape)],
        [set_spec, set_spec, wide_spec, wide_spec],
        [
            jax.ShapeDtypeStruct((pixels, 2 * LANES), F32), jax.ShapeDtypeStruct((pixels, 2 * LANES), BF16),
            jax.ShapeDtypeStruct((pixels, width), BF16), jax.ShapeDtypeStruct((pixels, width), BF16),
        ],
        flops=2 * pixels * 512 * width, bytes_moved=16 << 20, name="back_three",
    )(at, every, r3, r3b, gb3, y3, features, out_grad, grad_pooled, mk, ind, weight_three)
    ga_near = swap_lo(ga_send)
    ga_far = swap_hi((pick(ga_keep) + pick(ga_near).astype(F32)).astype(BF16))
    dz2, st2b = call(
        functools.partial(slope_kernel, 2, 3), per_half,
        [e_spec, r_spec, own_spec, own_spec, row_spec, row_spec, mk_spec], [row_spec, st_spec],
        [y_shape, st_shape], bytes_moved=4 << 20, name="slope_two",
    )(at, every, r2, ga_keep, ga_near, ga_far, y2, mk)
    r2b = spread(st2b, ALL, n_all)

    gb_keep, gb_send = call(
        conv_input_kernel, per_half,
        [e_spec, r_spec, r_spec, row_spec, row_spec, w2_spec, mk_spec], [row_spec, row_spec],
        [jax.ShapeDtypeStruct((half, 2 * LANES), F32), y_shape],
        flops=18 * half * 512 * 256, bytes_moved=6 << 20, name="conv_input",
    )(at, every, r2, r2b, dz2, y2, w2, mk)
    gb_near = swap_lo(gb_send)
    dz1, st1b = call(
        functools.partial(slope_kernel, 0, 2), per_half,
        [e_spec, r_spec, row_spec, row_spec, row_spec, mk_spec], [row_spec, st_spec],
        [y_shape, st_shape], bytes_moved=3 << 20, name="slope_one",
    )(at, every, r1, gb_keep, gb_near, y1, mk)
    dz1_near = swap_lo(dz1)
    dz1_far = swap_hi(dz1)
    r1b = spread(st1b, ALL, n_all)
    dz1_across = swap_lo(dz1_far)

    theirs = jnp.where(hi0, dz2[:, LANES:], dz2[:, :LANES])
    mine = jnp.where(hi0, dz2[:, :LANES], dz2[:, LANES:])
    dz2_far = swap_hi(theirs)
    lane_part = pl.BlockSpec((ROWS, LANES), lambda i, at: (i % per_half, 0))
    lane_pick = pl.BlockSpec((ROWS, LANES), lambda i, at: (i % per_half, at[0]))
    grad_two = call(
        functools.partial(conv_weight_kernel, per_half), steps,
        [e_spec, r_spec, r_spec, r_spec] + parts + [lane_part, lane_part, lane_pick, lane_pick, mk_spec],
        whole((9, 512, LANES)), jax.ShapeDtypeStruct((9, 512, LANES), BF16),
        scratch=[pltpu.VMEM((512, 9 * LANES), F32)],
        flops=18 * pixels * 512 * LANES, bytes_moved=8 << 20, name="conv_weight",
    )(at, every, r1, r2, r2b, y1, y1_near, y1_far, y1_across, mine, dz2_far, y2, y2_far, mk)

    gy1, grad_one = call(
        functools.partial(first_weight_kernel, per_half), steps,
        [e_spec, r_spec, r_spec] + parts + parts + [wide_spec, mk_spec],
        [rows_spec(4 * LANES), whole((4, width, LANES))],
        [jax.ShapeDtypeStruct((pixels, 4 * LANES), BF16), jax.ShapeDtypeStruct((4, width, LANES), BF16)],
        scratch=[pltpu.VMEM((width, 4 * LANES), F32)],
        flops=2 * pixels * 512 * width, bytes_moved=8 << 20, name="first_weight",
    )(at, every, r1, r1b, dz1, dz1_near, dz1_far, dz1_across, y1, y1_near, y1_far, y1_across, features, mk)
    grad_features = (dot_nt(gy1, w_first) + dz3.astype(F32)).astype(BF16)

    piece = width // n_wide
    sent = grad_one.reshape(4, n_wide, piece, LANES).transpose(1, 0, 2, 3).reshape(n_all, piece, LANES)
    got = lax.all_to_all(sent, ALL, 0, 0, tiled=True).astype(F32)
    got = jnp.sum(got.reshape(n_wide, 4, piece, LANES), axis=0).astype(BF16)
    grad_one = (
        spread(got, "wide", n_wide).reshape(n_wide, 4, piece, LANES)
        .transpose(1, 0, 2, 3).reshape(4 * width, LANES).astype(F32)
    )
    grad_two = lax.psum(grad_two, "wide").astype(F32).reshape(weight_two.shape)
    grad_three = dot_tn(a2, gy3).astype(BF16)
    grad_head = dot_tn(pooled.astype(BF16), grad_raw.astype(BF16)).astype(BF16)
    grad_three, grad_head = lax.psum((grad_three, grad_head), "wide")

    def own_sums(r):
        by = jnp.sum(r.reshape(n_wide, 2, 2, 2, 2, LANES), axis=(0, 1))
        both = lax.dynamic_index_in_dim(by, lo, 0, keepdims=False)
        both = lax.dynamic_index_in_dim(both, hi, 1, keepdims=False)
        return both[0], both[1]

    d_shift_one, d_gain_one = own_sums(r1b)
    d_shift_two, d_gain_two = own_sums(r2b)
    back_three = jnp.sum(r3b, axis=0)
    d_shift_three, d_gain_three = back_three[:4].reshape(-1), back_three[4:].reshape(-1)

    all_embed = spread(embedding, "wide", n_wide).reshape(-1, LANES)
    all_slot = every.reshape(n_wide, 4, 8, LANES)[:, 0, 5, :images].reshape(-1)
    bank_rows = memory_bank.shape[0]
    owner = all_slot.astype(jnp.int32) - lax.axis_index("wide") * bank_rows
    owned = (owner >= 0) & (owner < bank_rows)
    target = jnp.where(owned, owner, bank_rows)
    previous = jnp.take(memory_bank, jnp.minimum(target, bank_rows - 1), axis=0)
    mixed = 0.5 * previous + 0.5 * all_embed
    mixed = mixed * lax.rsqrt(jnp.sum(mixed * mixed, axis=1, keepdims=True) + EPS_EMBED)
    new_bank = memory_bank.at[target].set(mixed, mode="drop")

    return (
        out,
        embedding,
        grad_features,
        grad_one,
        d_gain_one,
        d_shift_one,
        grad_two,
        d_gain_two,
        d_shift_two,
        grad_three.astype(F32),
        d_gain_three,
        d_shift_three,
        grad_head.astype(F32),
        new_bank,
    )


def solution(mesh):
    n_wide, n_narrow = mesh.shape["wide"], mesh.shape["narrow"]
    split = Mesh(mesh.devices.reshape(n_wide, n_narrow // 2, 2), ALL)
    narrow = ("hi", "lo")
    in_specs = (
        P("wide", narrow),
        P("wide"),
        P("wide"),
        P("wide", None),
        P(None, narrow),
        P(narrow),
        P(narrow),
        P(None, None, None, narrow),
        P(narrow),
        P(narrow),
        P(None, narrow),
        P(narrow),
        P(narrow),
        P(narrow, None),
        P("wide", narrow),
        P("wide", None),
    )
    out_specs = (
        P("wide", narrow),
        P("wide", None),
        P("wide", narrow),
        P(None, narrow),
        P(narrow),
        P(narrow),
        P(None, None, None, narrow),
        P(narrow),
        P(narrow),
        P(None, narrow),
        P(narrow),
        P(narrow),
        P(narrow, None),
        P("wide", None),
    )
    return jax.shard_map(
        functools.partial(shards, n_wide),
        mesh=split,
        in_specs=in_specs,
        out_specs=out_specs,
        check_vma=False,
    )
```
